32 devices in a mesh: seq: 8 (over z, y), chan: 4 (over x, core).
Axes of the slice: x: 2, y: 2, z: 4, core: 2. Of those that a mesh axis runs over, the one named last changes fastest.
Arguments:
- tokens: bfloat16 [4096, 4096], P('seq', 'chan'), may hold values from -6 to 6
- grad_out: bfloat16 [4096, 4096], P('seq', 'chan'), may hold values from -0.125 to 0.125
- in_weight: bfloat16 [4096, 3, 256], P('seq', None, 'chan'), may hold values from -0.09375 to 0.09375
- out_weight: bfloat16 [4096, 256], P('seq', 'chan'), may hold values from -0.09375 to 0.09375
- conv_out: bfloat16 [4096, 256], P('seq', 'chan'), may hold values from -6 to 6
- residues: float32 [16, 128], P(None, 'chan'), may hold values from -1.5 to 1.5
- decay_length: float32 [16, 128], P(None, 'chan'), may hold values from 8 to 262144
Outputs:
- grad_in_weight: float32 [4096, 3, 256], P('seq', None, 'chan')
- grad_out_weight: float32 [4096, 256], P('seq', 'chan')
The draws below stay inside these ranges and needn't reach their ends.
All inputs are finite; a program needn't handle non-finite values.
Results may differ from the reference program's by a relative error of at most 0.0041.
Values may be sent and summed in bfloat16 or wider, within the bound.
A program may use at most 64 MiB of HBM per device.

```python
import math
import jax
import jax.numpy as jnp
from jax import lax

D = 4096
C = 256
MODES = 16
SEQ = 4096
FILTERS = 128


def strengthened(array, rng, source, target, blocks, factor):
    def block_of(position):
        return (jnp.arange(array.shape[position]) // (array.shape[position] // blocks)).reshape((-1,) + (1,) * (array.ndim - 1 - position))

    first = jax.random.permutation(rng, blocks)[block_of(target)]
    other_side = (block_of(target) + blocks // 2) % blocks
    return jnp.where((block_of(source) == first) | (block_of(source) == other_side), factor * array, array)


def steps_of(own_key, shape, split, smallest, top_value):
    loudness, own = 1.0, jax.random.fold_in(own_key, 6)
    for axis_at, blocks in split:
        draws = jnp.exp(jax.random.uniform(jax.random.fold_in(own, axis_at), (blocks,), jnp.float32, smallest / len(split), top_value / len(split)))
        loudness = loudness * jnp.repeat(draws, shape[axis_at] // blocks).reshape([-1 if axis == axis_at else 1 for axis in range(len(shape))])
    return loudness


def bell_draw(stream_key, dims, scale, bound, split=(), held_as=jnp.bfloat16):
    entries = scale * jax.random.normal(stream_key, dims, jnp.float32)
    if split:
        entries = entries * steps_of(stream_key, dims, split, -0.22, 0.18)
    return jnp.clip(entries, -bound, bound).astype(held_as)


def gaussian_with(rng, shape, deviation, most, split, heavy, dtype=jnp.bfloat16):
    array = deviation * jax.random.normal(rng, shape, jnp.float32)
    if split:
        array = array * steps_of(rng, shape, split, -0.22, 0.18)
    return jnp.clip(strengthened(array, jax.random.fold_in(rng, 3), *heavy), -most, most).astype(dtype)


def setup_inputs(seed: int = 0) -> dict:
    keys = jax.random.split(jax.random.key(seed), 8)
    return {
        "tokens": gaussian_with(keys[0], (SEQ, D), 1.0, 6.0, ((0, 8), (1, 4)), (0, 1, 8, 2.0)),
        "grad_out": gaussian_with(keys[1], (SEQ, D), SEQ ** -0.5, 0.125, ((0, 8), (1, 4)), (0, 1, 8, 2.0)),
        "in_weight": bell_draw(keys[2], (D, 3, C), D ** -0.5, 0.09375, ((0, 8), (2, 4))),
        "out_weight": bell_draw(keys[3], (D, C), D ** -0.5, 0.09375, ((0, 8), (1, 4))),
        "conv_out": bell_draw(keys[4], (SEQ, C), 1.0, 6.0, ((0, 8), (1, 4))),
        "residues": bell_draw(keys[5], (MODES, FILTERS), MODES ** -0.5, 1.5, ((1, 4),), jnp.float32),
        "decay_length": jnp.clip(jnp.exp(math.log(262144.0) - 10.3972077 * jax.random.uniform(keys[6], (MODES, FILTERS), jnp.float32) ** steps_of(keys[6], (MODES, FILTERS), ((1, 4),), -0.2, 0.2)), 8.0, 262144.0),
    }


def filter_taps(residues, decay_length):
    inverse_len = 1.0 / decay_length
    weight = residues * jnp.sqrt(-jnp.expm1(-2.0 * inverse_len))
    moments = jnp.arange(SEQ).astype(jnp.float32)

    def add_mode(running, inputs):
        mode_weight, mode_rate = inputs
        return (running + mode_weight[None, :] * jnp.exp(-moments[:, None] * mode_rate[None, :]), None)
    impulse, _ = lax.scan(add_mode, jnp.zeros((SEQ, FILTERS), jnp.float32), (weight, inverse_len))
    return impulse

def correlate(impulse, signal):
    paired = signal[:, 0::2] + 1j * signal[:, 1::2]
    spectrum = jnp.fft.fft(paired, n=2 * SEQ, axis=0)
    response = jnp.conj(jnp.fft.fft(impulse, n=2 * SEQ, axis=0))
    result = jnp.fft.ifft(spectrum * response, axis=0)[:SEQ]
    return jnp.stack([jnp.real(result), jnp.imag(result)], axis=2).reshape(SEQ, C)

def reference(tokens, grad_out, in_weight, out_weight, conv_out, residues, decay_length):
    projected = jnp.dot(tokens, in_weight.reshape(D, 3 * C), preferred_element_type=jnp.float32)
    streams = projected.astype(jnp.bfloat16).reshape(SEQ, 3, C)
    gate_first = streams[:, 0].astype(jnp.float32)
    gate_second = streams[:, 1].astype(jnp.float32)
    value_stream = streams[:, 2].astype(jnp.float32)
    conv_value = conv_out.astype(jnp.float32)
    gated = (gate_second * conv_value).astype(jnp.bfloat16)
    upstream = jnp.dot(grad_out, out_weight, preferred_element_type=jnp.float32)
    grad_second = (upstream * conv_value).astype(jnp.bfloat16)
    grad_conv = upstream * gate_second
    grad_source = correlate(filter_taps(residues, decay_length), grad_conv)
    grad_first = (grad_source * value_stream).astype(jnp.bfloat16)
    grad_value = (grad_source * gate_first).astype(jnp.bfloat16)
    grad_streams = jnp.stack([grad_first, grad_second, grad_value], axis=1).reshape(SEQ, 3 * C)
    grad_in = lax.dot_general(tokens, grad_streams, (((0,), (0,)), ((), ())), preferred_element_type=jnp.float32)
    grad_proj = lax.dot_general(grad_out, gated, (((0,), (0,)), ((), ())), preferred_element_type=jnp.float32)
    return (grad_in.reshape(D, 3, C), grad_proj)
```

```python
import functools
import math

import jax
import jax.numpy as jnp
from jax import lax
from jax.experimental import pallas as pl
from jax.experimental.pallas import tpu as pltpu
from jax.sharding import PartitionSpec as P

precise = lax.Precision.HIGHEST
MESH = pl.DeviceIdType.MESH


def remote(source, target, send_sem, recv_sem, device):
    return pltpu.make_async_remote_copy(
        src_ref=source,
        dst_ref=target,
        send_sem=send_sem,
        recv_sem=recv_sem,
        device_id=device,
        device_id_type=MESH,
    )


def greet(devices_seq, devices_chan, seq_wide):
    seq, chan = lax.axis_index("seq"), lax.axis_index("chan")
    barrier = pltpu.get_barrier_semaphore()
    count = 0
    if seq_wide == "all":

        def hello(step, carry):
            pl.semaphore_signal(
                barrier,
                inc=1,
                device_id=(lax.rem(seq + step, devices_seq), chan),
                device_id_type=MESH,
            )
            return carry

        lax.fori_loop(1, devices_seq, hello, 0)
        count += devices_seq - 1
    else:
        groups = devices_seq // 2

        def hello_group(step, carry):
            there = lax.rem(seq // 2 + step, groups) * 2 + seq % 2
            pl.semaphore_signal(barrier, inc=1, device_id=(there, chan), device_id_type=MESH)
            return carry

        lax.fori_loop(1, groups, hello_group, 0)
        pl.semaphore_signal(
            barrier, inc=1, device_id=(seq + 1 - 2 * (seq % 2), chan), device_id_type=MESH
        )
        count += groups
    if devices_chan:
        groups = devices_chan // 2
        for step in range(1, groups):
            there = lax.rem(chan // 2 + step, groups) * 2 + chan % 2
            pl.semaphore_signal(barrier, inc=1, device_id=(seq, there), device_id_type=MESH)
        pl.semaphore_signal(
            barrier, inc=1, device_id=(seq, chan + 1 - 2 * (chan % 2)), device_id_type=MESH
        )
        count += groups
    pl.semaphore_wait(barrier, count)


def gather_kernel(
    devices_seq,
    devices_chan,
    tokens,
    grads,
    weights,
    all_tokens,
    all_grads,
    all_weights,
    keep_sem,
    chan_send,
    chan_recv,
    chan_pass,
    chan_passed,
    seq_send,
    seq_recv,
    seq_pass,
    seq_passed,
):
    seq, chan = lax.axis_index("seq"), lax.axis_index("chan")
    seq_groups, chan_groups = devices_seq // 2, devices_chan // 2
    seq_pair = (seq + 1 - 2 * (seq % 2), chan)
    chan_pair = (seq, chan + 1 - 2 * (chan % 2))
    columns = tokens.shape[1]
    rows = weights.shape[0]
    greet(devices_seq, devices_chan, "pairs")

    def block(ref, index):
        return ref.at[:, pl.ds(pl.multiple_of(index * columns, columns), columns)]

    def piece(index):
        return all_weights.at[pl.ds(pl.multiple_of(index * rows, rows), rows)]

    def chan_member(step, parity):
        return lax.rem(chan // 2 - step + chan_groups, chan_groups) * 2 + parity

    def seq_member(step, parity):
        return lax.rem(seq // 2 - step + seq_groups, seq_groups) * 2 + parity

    pairs = ((tokens, all_tokens), (grads, all_grads))

    def chan_copy(array, step):
        own, whole = pairs[array]
        there = lax.rem(chan // 2 + step, chan_groups) * 2 + chan % 2
        return remote(
            own,
            block(whole, chan),
            chan_send.at[array, step],
            chan_recv.at[array, step],
            (seq, there),
        )

    def chan_forward(array, step):
        own, whole = pairs[array]
        here = chan_member(step, chan % 2)
        return remote(
            own if step == 0 else block(whole, here),
            block(whole, here),
            chan_pass.at[array, step],
            chan_passed.at[array, step],
            chan_pair,
        )

    def seq_copy(step):
        there = lax.rem(seq // 2 + step, seq_groups) * 2 + seq % 2
        return remote(weights, piece(seq), seq_send.at[step], seq_recv.at[step], (there, chan))

    def seq_forward(step):
        here = seq_member(step, seq % 2)
        return remote(piece(here), piece(here), seq_pass.at[step], seq_passed.at[step], seq_pair)

    own_piece = remote(weights, piece(seq), seq_pass.at[0], seq_passed.at[0], seq_pair)

    def each(call):
        def body(step, carry):
            call(step)
            return carry

        lax.fori_loop(1, seq_groups, body, 0)

    for array in range(2):
        for step in range(1, chan_groups):
            chan_copy(array, step).start()
    each(lambda step: seq_copy(step).start())
    own_piece.start()
    for array in range(2):
        chan_forward(array, 0).start()
    keeps = [
        pltpu.make_async_copy(tokens, block(all_tokens, chan), keep_sem.at[0]),
        pltpu.make_async_copy(grads, block(all_grads, chan), keep_sem.at[1]),
        pltpu.make_async_copy(weights, piece(seq), keep_sem.at[2]),
    ]
    for keep in keeps:
        keep.start()

    def pass_on(step):
        seq_copy(step).wait_recv()
        seq_forward(step).start()

    each(pass_on)
    for array in range(2):
        for step in range(1, chan_groups):
            chan_copy(array, step).wait_recv()
            chan_forward(array, step).start()
    for keep in keeps:
        keep.wait()
    own_piece.wait()

    def finish(step):
        seq_copy(step).wait_send()
        seq_forward(step).wait()

    each(finish)
    for array in range(2):
        for step in range(chan_groups):
            chan_forward(array, step).wait()
        for step in range(1, chan_groups):
            chan_copy(array, step).wait_send()


def gathered(tokens, grads, weights):
    devices_seq, devices_chan = lax.axis_size("seq"), lax.axis_size("chan")
    dma = pltpu.SemaphoreType.DMA
    seq_groups, chan_groups = devices_seq // 2, devices_chan // 2
    vmem, anywhere = pl.BlockSpec(memory_space=pltpu.VMEM), pl.BlockSpec(memory_space=pl.ANY)
    wide = jax.ShapeDtypeStruct((tokens.shape[0], tokens.shape[1] * devices_chan), tokens.dtype)
    tall = jax.ShapeDtypeStruct((weights.shape[0] * devices_seq, weights.shape[1]), weights.dtype)
    return pl.pallas_call(
        functools.partial(gather_kernel, devices_seq, devices_chan),
        out_shape=(wide, wide, tall),
        in_specs=[vmem] * 3,
        out_specs=(anywhere,) * 3,
        scratch_shapes=[dma((3,))]
        + [dma((2, chan_groups))] * 4
        + [dma((seq_groups,))] * 4,
        compiler_params=pltpu.CompilerParams(collective_id=0, has_side_effects=True),
        name="gather_inputs",
    )(tokens, grads, weights)


def states_kernel(devices_seq, own, whole, send, recv):
    seq, chan = lax.axis_index("seq"), lax.axis_index("chan")
    greet(devices_seq, 0, "all")

    def copy(step):
        there = lax.rem(seq + step, devices_seq)
        return remote(own, whole.at[seq], send.at[step], recv.at[step], (there, chan))

    def start(step, carry):
        copy(step).start()
        return carry

    def wait(step, carry):
        copy(step).wait()
        return carry

    lax.fori_loop(1, devices_seq, start, 0)
    whole[seq] = own[...]
    lax.fori_loop(1, devices_seq, wait, 0)


def gathered_states(state):
    devices_seq = lax.axis_size("seq")
    vmem = pl.BlockSpec(memory_space=pltpu.VMEM)
    return pl.pallas_call(
        functools.partial(states_kernel, devices_seq),
        out_shape=jax.ShapeDtypeStruct((devices_seq,) + state.shape, state.dtype),
        in_specs=[vmem],
        out_specs=vmem,
        scratch_shapes=[pltpu.SemaphoreType.DMA((devices_seq,))] * 2,
        compiler_params=pltpu.CompilerParams(collective_id=1, has_side_effects=True),
        name="gather_states",
    )(state)


def reduce_kernel(
    devices_seq, parts, total, near, paired, far, pair_send, pair_recv, far_send, far_recv
):
    seq, chan = lax.axis_index("seq"), lax.axis_index("chan")
    groups = devices_seq // 2
    group, parity = seq // 2, seq % 2
    greet(devices_seq, 0, "pairs")

    def member(step):
        return lax.rem(group + step, groups)

    def pair_copy(step):
        return remote(
            parts.at[member(step) * 2 + 1 - parity],
            near.at[step],
            pair_send.at[step],
            pair_recv.at[step],
            (group * 2 + 1 - parity, chan),
        )

    def far_copy(step):
        return remote(
            paired.at[step],
            far.at[step],
            far_send.at[step],
            far_recv.at[step],
            (member(step) * 2 + parity, chan),
        )

    def each(call):
        def body(step, carry):
            call(step)
            return carry

        lax.fori_loop(1, groups, body, 0)

    def pair_sum(step):
        own = parts[member(step) * 2 + parity].astype(jnp.float32)
        return own + near[step].astype(jnp.float32)

    each(lambda step: pair_copy(step).start())
    pair_copy(0).start()

    def pass_on(step):
        pair_copy(step).wait_recv()
        paired[step] = pair_sum(step).astype(paired.dtype)
        far_copy(step).start()

    each(pass_on)
    pair_copy(0).wait_recv()
    total[...] = pair_sum(0)

    def collect(step):
        far_copy(step).wait_recv()
        total[...] += far[step].astype(jnp.float32)

    each(collect)

    def finish(step):
        pair_copy(step).wait_send()
        far_copy(step).wait_send()

    each(finish)
    pair_copy(0).wait_send()


def reduced(parts):
    devices_seq = lax.axis_size("seq")
    groups = devices_seq // 2
    shape = parts.shape[1:]
    vmem = pl.BlockSpec(memory_space=pltpu.VMEM)
    return pl.pallas_call(
        functools.partial(reduce_kernel, devices_seq),
        out_shape=jax.ShapeDtypeStruct(shape, jnp.float32),
        in_specs=[vmem],
        out_specs=vmem,
        scratch_shapes=[pltpu.VMEM((groups,) + shape, parts.dtype)] * 3
        + [pltpu.SemaphoreType.DMA((groups,))] * 4,
        compiler_params=pltpu.CompilerParams(collective_id=2, has_side_effects=True),
        name="reduce_owned",
    )(parts)


def correlate(signal, residues, decay_length):
    rows, channels = signal.shape
    devices_seq = lax.axis_size("seq")
    position = lax.axis_index("seq")
    chunk = min(64, rows)
    chunks = rows // chunk
    per_filter = channels // residues.shape[1]
    rate = jnp.repeat(1.0 / decay_length, per_filter, axis=1)
    weight = jnp.repeat(residues, per_filter, axis=1) * jnp.sqrt(-jnp.expm1(-2.0 * rate))
    offset = jnp.arange(chunk, dtype=jnp.float32)
    exponent = rate.T[:, :, None] * offset
    grow = weight.T[:, :, None] * jnp.exp(exponent)
    fall = jnp.exp(-exponent)
    later = jnp.arange(chunk)[None, :] >= jnp.arange(chunk)[:, None]
    taps = jnp.einsum("cri,crj->cij", grow, fall, precision=precise)
    taps = jnp.where(later, taps, 0.0)
    pieces = signal.reshape(chunks, chunk, channels).transpose(2, 1, 0)
    both = jnp.einsum(
        "cij,cjn->cin", jnp.concatenate([taps, fall], axis=1), pieces, precision=precise
    )
    inner, sums = both[:, :chunk], both[:, chunk:]
    step = jnp.exp(-chunk * rate).T
    state = jnp.zeros_like(step)
    entering = []
    for index in reversed(range(chunks)):
        entering.append(step * state)
        state = sums[:, :, index] + step * state
    entering = jnp.stack(entering[::-1], axis=2)
    states = gathered_states(state)
    gap = (jnp.arange(devices_seq) - position - 1).astype(jnp.float32) * rows
    scale = jnp.where(
        gap[:, None, None] >= 0.0,
        jnp.exp(-jnp.maximum(gap, 0.0)[:, None, None] * rate.T),
        0.0,
    )
    following = jnp.sum(scale * states, axis=0)
    reach = (chunks - jnp.arange(chunks)).astype(jnp.float32) * chunk
    entering = entering + following[:, :, None] * jnp.exp(-rate.T[:, :, None] * reach)
    outer = jnp.einsum("cri,crn->cin", grow, entering, precision=precise)
    return (inner + outer).transpose(2, 1, 0).reshape(rows, channels)


def local(tokens, grad_out, in_weight, out_weight, conv_out, residues, decay_length):
    local_rows = tokens.shape[0]
    channels = out_weight.shape[1]
    owned_rows = in_weight.shape[0]
    weights = jnp.concatenate([in_weight.reshape(owned_rows, 3 * channels), out_weight], axis=1)
    full_tokens, full_grads, full_weights = gathered(tokens, grad_out, weights)
    projected = jnp.dot(
        full_tokens, full_weights[:, : 3 * channels], preferred_element_type=jnp.float32
    )
    upstream = jnp.dot(
        full_grads, full_weights[:, 3 * channels :], preferred_element_type=jnp.float32
    )
    streams = projected.astype(jnp.bfloat16).astype(jnp.float32)
    gate_first = streams[:, :channels]
    gate_second = streams[:, channels : 2 * channels]
    value_stream = streams[:, 2 * channels :]
    conv_value = conv_out.astype(jnp.float32)
    gated = (gate_second * conv_value).astype(jnp.bfloat16)
    grad_second = (upstream * conv_value).astype(jnp.bfloat16)
    grad_conv = upstream * gate_second
    grad_source = correlate(grad_conv, residues, decay_length)
    grad_first = (grad_source * value_stream).astype(jnp.bfloat16)
    grad_value = (grad_source * gate_first).astype(jnp.bfloat16)
    grad_streams = jnp.concatenate([grad_first, grad_second, grad_value], axis=1)
    inward = lax.dot_general(
        full_tokens, grad_streams, (((0,), (0,)), ((), ())), preferred_element_type=jnp.float32
    )
    outward = lax.dot_general(
        full_grads, gated, (((0,), (0,)), ((), ())), preferred_element_type=jnp.float32
    )
    parts = jnp.concatenate([inward, outward], axis=1).astype(jnp.bfloat16)
    owned = reduced(parts.reshape(-1, owned_rows, 4 * channels))
    grad_in = owned[:, : 3 * channels].reshape(owned_rows, 3, channels)
    grad_proj = owned[:, 3 * channels :]
    return (grad_in, grad_proj)


def solution(mesh):
    return jax.shard_map(
        local,
        mesh=mesh,
        in_specs=(
            P("seq", "chan"),
            P("seq", "chan"),
            P("seq", None, "chan"),
            P("seq", "chan"),
            P("seq", "chan"),
            P(None, "chan"),
            P(None, "chan"),
        ),
        out_specs=(P("seq", None, "chan"), P("seq", "chan")),
        check_vma=False,
    )
```

```python
import functools
import math

import jax
import jax.numpy as jnp
from jax import lax
from jax.experimental import pallas as pl
from jax.experimental.pallas import tpu as pltpu
from jax.sharding import PartitionSpec as P

precise = lax.Precision.HIGHEST
MESH = pl.DeviceIdType.MESH


def remote(source, target, send_sem, recv_sem, device):
    return pltpu.make_async_remote_copy(
        src_ref=source,
        dst_ref=target,
        send_sem=send_sem,
        recv_sem=recv_sem,
        device_id=device,
        device_id_type=MESH,
    )


def greet(devices_seq, devices_chan, seq_wide):
    seq, chan = lax.axis_index("seq"), lax.axis_index("chan")
    barrier = pltpu.get_barrier_semaphore()
    count = 0
    if seq_wide == "all":

        def hello(step, carry):
            pl.semaphore_signal(
                barrier,
                inc=1,
                device_id=(lax.rem(seq + step, devices_seq), chan),
                device_id_type=MESH,
            )
            return carry

        lax.fori_loop(1, devices_seq, hello, 0)
        count += devices_seq - 1
    else:
        groups = devices_seq // 2

        def hello_group(step, carry):
            there = lax.rem(seq // 2 + step, groups) * 2 + seq % 2
            pl.semaphore_signal(barrier, inc=1, device_id=(there, chan), device_id_type=MESH)
            return carry

        lax.fori_loop(1, groups, hello_group, 0)
        pl.semaphore_signal(
            barrier, inc=1, device_id=(seq + 1 - 2 * (seq % 2), chan), device_id_type=MESH
        )
        count += groups
    if devices_chan:
        groups = devices_chan // 2
        for step in range(1, groups):
            there = lax.rem(chan // 2 + step, groups) * 2 + chan % 2
            pl.semaphore_signal(barrier, inc=1, device_id=(seq, there), device_id_type=MESH)
        pl.semaphore_signal(
            barrier, inc=1, device_id=(seq, chan + 1 - 2 * (chan % 2)), device_id_type=MESH
        )
        count += groups
    pl.semaphore_wait(barrier, count)


def gather_kernel(
    devices_seq,
    devices_chan,
    tokens,
    grads,
    weights,
    all_tokens,
    all_grads,
    all_weights,
    keep_sem,
    chan_send,
    chan_recv,
    chan_pass,
    chan_passed,
    seq_send,
    seq_recv,
    seq_pass,
    seq_passed,
):
    seq, chan = lax.axis_index("seq"), lax.axis_index("chan")
    seq_groups, chan_groups = devices_seq // 2, devices_chan // 2
    seq_pair = (seq + 1 - 2 * (seq % 2), chan)
    chan_pair = (seq, chan + 1 - 2 * (chan % 2))
    columns = tokens.shape[1]
    rows = weights.shape[0]
    greet(devices_seq, devices_chan, "pairs")

    def block(ref, index):
        return ref.at[:, pl.ds(pl.multiple_of(index * columns, columns), columns)]

    def piece(index):
        return all_weights.at[pl.ds(pl.multiple_of(index * rows, rows), rows)]

    def chan_member(step, parity):
        return lax.rem(chan // 2 - step + chan_groups, chan_groups) * 2 + parity

    def seq_member(step, parity):
        return lax.rem(seq // 2 - step + seq_groups, seq_groups) * 2 + parity

    pairs = ((tokens, all_tokens), (grads, all_grads))

    def chan_copy(array, step):
        own, whole = pairs[array]
        there = lax.rem(chan // 2 + step, chan_groups) * 2 + chan % 2
        return remote(
            own,
            block(whole, chan),
            chan_send.at[array, step],
            chan_recv.at[array, step],
            (seq, there),
        )

    def chan_forward(array, step):
        own, whole = pairs[array]
        here = chan_member(step, chan % 2)
        return remote(
            own if step == 0 else block(whole, here),
            block(whole, here),
            chan_pass.at[array, step],
            chan_passed.at[array, step],
            chan_pair,
        )

    def seq_copy(step):
        there = lax.rem(seq // 2 + step, seq_groups) * 2 + seq % 2
        return remote(weights, piece(seq), seq_send.at[step], seq_recv.at[step], (there, chan))

    def seq_forward(step):
        here = seq_member(step, seq % 2)
        return remote(piece(here), piece(here), seq_pass.at[step], seq_passed.at[step], seq_pair)

    own_piece = remote(weights, piece(seq), seq_pass.at[0], seq_passed.at[0], seq_pair)

    def each(call):
        def body(step, carry):
            call(step)
            return carry

        lax.fori_loop(1, seq_groups, body, 0)

    for array in range(2):
        for step in range(1, chan_groups):
            chan_copy(array, step).start()
    each(lambda step: seq_copy(step).start())
    own_piece.start()
    for array in range(2):
        chan_forward(array, 0).start()
    keeps = [
        pltpu.make_async_copy(tokens, block(all_tokens, chan), keep_sem.at[0]),
        pltpu.make_async_copy(grads, block(all_grads, chan), keep_sem.at[1]),
        pltpu.make_async_copy(weights, piece(seq), keep_sem.at[2]),
    ]
    for keep in keeps:
        keep.start()

    def pass_on(step):
        seq_copy(step).wait_recv()
        seq_forward(step).start()

    each(pass_on)
    for array in range(2):
        for step in range(1, chan_groups):
            chan_copy(array, step).wait_recv()
            chan_forward(array, step).start()
    for keep in keeps:
        keep.wait()
    own_piece.wait()

    def finish(step):
        seq_copy(step).wait_send()
        seq_forward(step).wait()

    each(finish)
    for array in range(2):
        for step in range(chan_groups):
            chan_forward(array, step).wait()
        for step in range(1, chan_groups):
            chan_copy(array, step).wait_send()


def gathered(tokens, grads, weights):
    devices_seq, devices_chan = lax.axis_size("seq"), lax.axis_size("chan")
    dma = pltpu.SemaphoreType.DMA
    seq_groups, chan_groups = devices_seq // 2, devices_chan // 2
    vmem, anywhere = pl.BlockSpec(memory_space=pltpu.VMEM), pl.BlockSpec(memory_space=pl.ANY)
    wide = jax.ShapeDtypeStruct((tokens.shape[0], tokens.shape[1] * devices_chan), tokens.dtype)
    tall = jax.ShapeDtypeStruct((weights.shape[0] * devices_seq, weights.shape[1]), weights.dtype)
    return pl.pallas_call(
        functools.partial(gather_kernel, devices_seq, devices_chan),
        out_shape=(wide, wide, tall),
        in_specs=[vmem] * 3,
        out_specs=(anywhere,) * 3,
        scratch_shapes=[dma((3,))]
        + [dma((2, chan_groups))] * 4
        + [dma((seq_groups,))] * 4,
        compiler_params=pltpu.CompilerParams(collective_id=0, has_side_effects=True),
        name="gather_inputs",
    )(tokens, grads, weights)


def reduce_kernel(
    devices_seq,
    tile,
    state,
    rate,
    weight,
    inner,
    value,
    gate,
    early_in,
    early_out,
    tokens_hbm,
    grads_hbm,
    total,
    tokens,
    grads,
    states,
    late,
    parts,
    near,
    paired,
    far,
    load_sem,
    state_send,
    state_recv,
    pair_send,
    pair_recv,
    far_send,
    far_recv,
):
    seq, chan = lax.axis_index("seq"), lax.axis_index("chan")
    groups = devices_seq // 2
    group, parity = seq // 2, seq % 2
    rows, channels = inner.shape
    owned = near.shape[2]
    loads = [
        pltpu.make_async_copy(tokens_hbm, tokens, load_sem.at[0]),
        pltpu.make_async_copy(grads_hbm, grads, load_sem.at[1]),
    ]
    for load in loads:
        load.start()
    greet(devices_seq, 0, "all")

    def loop(start, stop, call):
        def body(step, carry):
            call(step)
            return carry

        lax.fori_loop(start, stop, body, 0)

    def state_copy(step):
        there = lax.rem(seq + step, devices_seq)
        return remote(
            state, states.at[step], state_send.at[step], state_recv.at[step], (there, chan)
        )

    def member(step):
        return lax.rem(group + step, groups)

    def piece(half, index):
        return parts.at[half, pl.ds(pl.multiple_of(index * owned, owned), owned)]

    def pair_copy(half, step):
        return remote(
            piece(half, member(step) * 2 + 1 - parity),
            near.at[half, step],
            pair_send.at[half, step],
            pair_recv.at[half, step],
            (group * 2 + 1 - parity, chan),
        )

    def far_copy(half, step):
        return remote(
            paired.at[half, step],
            far.at[half, step],
            far_send.at[half, step],
            far_recv.at[half, step],
            (member(step) * 2 + parity, chan),
        )

    def summed(left, right):
        return lax.dot_general(
            left, right, (((0,), (0,)), ((), ())), preferred_element_type=jnp.float32
        )

    def span(index):
        return pl.ds(pl.multiple_of(index * tile, tile), tile)

    loop(1, devices_seq, lambda step: state_copy(step).start())
    for load in loads:
        load.wait()

    def early_tile(index):
        product = summed(tokens[:, span(index)], early_in[...])
        product += summed(grads[:, span(index)], early_out[...])
        parts[0, span(index)] = product.astype(parts.dtype)

    loop(0, tokens.shape[1] // tile, early_tile)
    loop(1, groups, lambda step: pair_copy(0, step).start())
    pair_copy(0, 0).start()

    def absorb(step, following):
        state_copy(step).wait_recv()
        gap = lax.rem(seq - step + devices_seq, devices_seq) - seq - 1
        reach = (jnp.maximum(gap, 0) * rows).astype(jnp.float32)
        present = (gap >= 0).astype(jnp.float32)
        return following + present * states[step] * jnp.exp(-reach * rate[...])

    following = lax.fori_loop(1, devices_seq, absorb, jnp.zeros(rate.shape, jnp.float32))
    entering = weight[...] * following
    rates = rate[...]
    band = math.gcd(rows, 64)

    def source_rows(index):
        here = pl.ds(pl.multiple_of(index * band, band), band)
        position = lax.broadcasted_iota(jnp.int32, (band, channels), 0) + index * band
        reach = (rows - position).astype(jnp.float32)
        source = inner[here]
        for mode in range(rates.shape[0]):
            source += entering[mode : mode + 1] * jnp.exp(-reach * rates[mode : mode + 1])
        late[here] = jnp.concatenate([source * value[here], source * gate[here]], axis=1).astype(
            late.dtype
        )

    loop(0, rows // band, source_rows)

    def late_tile(index):
        parts[1, span(index)] = summed(tokens[:, span(index)], late[...]).astype(parts.dtype)

    loop(0, tokens.shape[1] // tile, late_tile)
    loop(1, groups, lambda step: pair_copy(1, step).start())
    pair_copy(1, 0).start()

    def pair_sum(half, step):
        own = piece(half, member(step) * 2 + parity)[...].astype(jnp.float32)
        return own + near[half, step].astype(jnp.float32)

    for half in range(2):

        def pass_on(step):
            pair_copy(half, step).wait_recv()
            paired[half, step] = pair_sum(half, step).astype(paired.dtype)
            far_copy(half, step).start()

        loop(1, groups, pass_on)
    for half in range(2):
        pair_copy(half, 0).wait_recv()
        total[half] = pair_sum(half, 0)

        def collect(step):
            far_copy(half, step).wait_recv()
            total[half] += far[half, step].astype(jnp.float32)

        loop(1, groups, collect)

        def finish(step):
            pair_copy(half, step).wait_send()
            far_copy(half, step).wait_send()

        loop(1, groups, finish)
        pair_copy(half, 0).wait_send()
    loop(1, devices_seq, lambda step: state_copy(step).wait_send())


def reduced(state, rate, weight, inner, value, gate, early_in, early_out, tokens, grads, owned):
    devices_seq = lax.axis_size("seq")
    groups = devices_seq // 2
    rows, channels = inner.shape
    width = tokens.shape[1]
    wide = 2 * channels
    vmem, anywhere = pl.BlockSpec(memory_space=pltpu.VMEM), pl.BlockSpec(memory_space=pl.ANY)
    dma, half_type = pltpu.SemaphoreType.DMA, tokens.dtype
    return pl.pallas_call(
        functools.partial(reduce_kernel, devices_seq, math.gcd(width, 512)),
        out_shape=jax.ShapeDtypeStruct((2, owned, wide), jnp.float32),
        in_specs=[vmem] * 8 + [anywhere] * 2,
        out_specs=vmem,
        scratch_shapes=[pltpu.VMEM(tokens.shape, half_type)] * 2
        + [pltpu.VMEM((devices_seq,) + state.shape, jnp.float32)]
        + [pltpu.VMEM((rows, wide), half_type), pltpu.VMEM((2, width, wide), half_type)]
        + [pltpu.VMEM((2, groups, owned, wide), half_type)] * 3
        + [dma((2,)), dma((devices_seq,)), dma((devices_seq,))]
        + [dma((2, groups))] * 4,
        compiler_params=pltpu.CompilerParams(collective_id=1, has_side_effects=True),
        name="reduce_owned",
    )(state, rate, weight, inner, value, gate, early_in, early_out, tokens, grads)


def correlate_block(signal, residues, decay_length):
    rows, channels = signal.shape
    chunk = min(64, rows)
    chunks = rows // chunk
    per_filter = channels // residues.shape[1]
    rate = jnp.repeat(1.0 / decay_length, per_filter, axis=1)
    weight = jnp.repeat(residues, per_filter, axis=1) * jnp.sqrt(-jnp.expm1(-2.0 * rate))
    offset = jnp.arange(chunk, dtype=jnp.float32)
    exponent = rate.T[:, :, None] * offset
    grow = weight.T[:, :, None] * jnp.exp(exponent)
    fall = jnp.exp(-exponent)
    later = jnp.arange(chunk)[None, :] >= jnp.arange(chunk)[:, None]
    taps = jnp.einsum("cri,crj->cij", grow, fall, precision=precise)
    taps = jnp.where(later, taps, 0.0)
    pieces = signal.reshape(chunks, chunk, channels).transpose(2, 1, 0)
    both = jnp.einsum(
        "cij,cjn->cin", jnp.concatenate([taps, fall], axis=1), pieces, precision=precise
    )
    inner, sums = both[:, :chunk], both[:, chunk:]
    step = jnp.exp(-chunk * rate).T
    state = jnp.zeros_like(step)
    entering = []
    for index in reversed(range(chunks)):
        entering.append(step * state)
        state = sums[:, :, index] + step * state
    entering = jnp.stack(entering[::-1], axis=2)
    outer = jnp.einsum("cri,crn->cin", grow, entering, precision=precise)
    return (inner + outer).transpose(2, 1, 0).reshape(rows, channels), state.T, rate, weight


def local(tokens, grad_out, in_weight, out_weight, conv_out, residues, decay_length):
    local_rows = tokens.shape[0]
    channels = out_weight.shape[1]
    owned_rows = in_weight.shape[0]
    weights = jnp.concatenate([in_weight.reshape(owned_rows, 3 * channels), out_weight], axis=1)
    full_tokens, full_grads, full_weights = gathered(tokens, grad_out, weights)
    projected = jnp.dot(
        full_tokens, full_weights[:, : 3 * channels], preferred_element_type=jnp.float32
    )
    upstream = jnp.dot(
        full_grads, full_weights[:, 3 * channels :], preferred_element_type=jnp.float32
    )
    streams = lax.reduce_precision(projected, exponent_bits=8, mantissa_bits=7)
    gate_first = streams[:, :channels]
    gate_second = streams[:, channels : 2 * channels]
    value_stream = streams[:, 2 * channels :]
    conv_value = conv_out.astype(jnp.float32)
    gated = (gate_second * conv_value).astype(jnp.bfloat16)
    grad_second = (upstream * conv_value).astype(jnp.bfloat16)
    grad_conv = upstream * gate_second
    inner, state, rate, weight = correlate_block(grad_conv, residues, decay_length)
    blank = jnp.zeros_like(gated)
    owned = reduced(
        state,
        rate,
        weight,
        inner,
        value_stream,
        gate_first,
        jnp.concatenate([grad_second, blank], axis=1),
        jnp.concatenate([blank, gated], axis=1),
        full_tokens,
        full_grads,
        owned_rows,
    )
    grad_in = jnp.stack(
        [owned[1, :, :channels], owned[0, :, :channels], owned[1, :, channels:]], axis=1
    )
    return (grad_in, owned[0, :, channels:])


def solution(mesh):
    return jax.shard_map(
        local,
        mesh=mesh,
        in_specs=(
            P("seq", "chan"),
            P("seq", "chan"),
            P("seq", None, "chan"),
            P("seq", "chan"),
            P("seq", "chan"),
            P(None, "chan"),
            P(None, "chan"),
        ),
        out_specs=(P("seq", None, "chan"), P("seq", "chan")),
        check_vma=False,
    )
```

```python
import functools
import math

import jax
import jax.numpy as jnp
from jax import lax
from jax.experimental import pallas as pl
from jax.experimental.pallas import tpu as pltpu
from jax.sharding import PartitionSpec as P

precise = lax.Precision.HIGHEST
MESH = pl.DeviceIdType.MESH


def remote(source, target, send_sem, recv_sem, device):
    return pltpu.make_async_remote_copy(
        src_ref=source,
        dst_ref=target,
        send_sem=send_sem,
        recv_sem=recv_sem,
        device_id=device,
        device_id_type=MESH,
    )


def greet(devices_seq, devices_chan, seq_wide):
    seq, chan = lax.axis_index("seq"), lax.axis_index("chan")
    barrier = pltpu.get_barrier_semaphore()
    count = 0
    if seq_wide == "all":

        def hello(step, carry):
            pl.semaphore_signal(
                barrier,
                inc=1,
                device_id=(lax.rem(seq + step, devices_seq), chan),
                device_id_type=MESH,
            )
            return carry

        lax.fori_loop(1, devices_seq, hello, 0)
        count += devices_seq - 1
    else:
        groups = devices_seq // 2

        def hello_group(step, carry):
            there = lax.rem(seq // 2 + step, groups) * 2 + seq % 2
            pl.semaphore_signal(barrier, inc=1, device_id=(there, chan), device_id_type=MESH)
            return carry

        lax.fori_loop(1, groups, hello_group, 0)
        pl.semaphore_signal(
            barrier, inc=1, device_id=(seq + 1 - 2 * (seq % 2), chan), device_id_type=MESH
        )
        count += groups
    if devices_chan:
        groups = devices_chan // 2
        for step in range(1, groups):
            there = lax.rem(chan // 2 + step, groups) * 2 + chan % 2
            pl.semaphore_signal(barrier, inc=1, device_id=(seq, there), device_id_type=MESH)
        pl.semaphore_signal(
            barrier, inc=1, device_id=(seq, chan + 1 - 2 * (chan % 2)), device_id_type=MESH
        )
        count += groups
    pl.semaphore_wait(barrier, count)


def gather_kernel(
    devices_seq,
    devices_chan,
    tokens,
    grads,
    weights,
    tokens_out,
    grads_out,
    projected,
    upstream,
    all_tokens,
    all_grads,
    all_weights,
    keep_sem,
    store_sem,
    chan_send,
    chan_recv,
    chan_pass,
    chan_passed,
    seq_send,
    seq_recv,
    seq_pass,
    seq_passed,
):
    seq, chan = lax.axis_index("seq"), lax.axis_index("chan")
    seq_groups, chan_groups = devices_seq // 2, devices_chan // 2
    seq_pair = (seq + 1 - 2 * (seq % 2), chan)
    chan_pair = (seq, chan + 1 - 2 * (chan % 2))
    columns = tokens.shape[1]
    rows = weights.shape[0]
    greet(devices_seq, devices_chan, "pairs")

    def block(ref, lines, index):
        return ref.at[lines, pl.ds(pl.multiple_of(index * columns, columns), columns)]

    def piece(index):
        return all_weights.at[pl.ds(pl.multiple_of(index * rows, rows), rows)]

    def chan_member(step, parity):
        return lax.rem(chan // 2 - step + chan_groups, chan_groups) * 2 + parity

    def seq_member(step, parity):
        return lax.rem(seq // 2 - step + seq_groups, seq_groups) * 2 + parity

    height = tokens.shape[0] // 2
    parts = [
        (own, whole, out, pl.ds(half * height, height))
        for own, whole, out in ((tokens, all_tokens, tokens_out), (grads, all_grads, grads_out))
        for half in range(2)
    ]

    def chan_copy(array, step):
        own, whole, _, lines = parts[array]
        there = lax.rem(chan // 2 + step, chan_groups) * 2 + chan % 2
        return remote(
            own.at[lines],
            block(whole, lines, chan),
            chan_send.at[array, step],
            chan_recv.at[array, step],
            (seq, there),
        )

    def chan_forward(array, step):
        own, whole, _, lines = parts[array]
        here = chan_member(step, chan % 2)
        return remote(
            own.at[lines] if step == 0 else block(whole, lines, here),
            block(whole, lines, here),
            chan_pass.at[array, step],
            chan_passed.at[array, step],
            chan_pair,
        )

    def seq_copy(step):
        there = lax.rem(seq // 2 + step, seq_groups) * 2 + seq % 2
        return remote(weights, piece(seq), seq_send.at[step], seq_recv.at[step], (there, chan))

    def seq_forward(step):
        here = seq_member(step, seq % 2)
        return remote(piece(here), piece(here), seq_pass.at[step], seq_passed.at[step], seq_pair)

    own_piece = remote(weights, piece(seq), seq_pass.at[0], seq_passed.at[0], seq_pair)

    def each(call):
        def body(step, carry):
            call(step)
            return carry

        lax.fori_loop(1, seq_groups, body, 0)

    def store(array):
        _, whole, out, lines = parts[array]
        return pltpu.make_async_copy(whole.at[lines], out.at[lines], store_sem.at[array])

    for array in range(4):
        for step in range(1, chan_groups):
            chan_copy(array, step).start()
    each(lambda step: seq_copy(step).start())
    own_piece.start()
    for array in range(4):
        chan_forward(array, 0).start()
    keeps = [pltpu.make_async_copy(weights, piece(seq), keep_sem.at[4])]
    for array, (own, whole, _, lines) in enumerate(parts):
        keeps.append(
            pltpu.make_async_copy(own.at[lines], block(whole, lines, chan), keep_sem.at[array])
        )
    for keep in keeps:
        keep.start()

    def pass_on(step):
        seq_copy(step).wait_recv()
        seq_forward(step).start()

    def pass_part(array):
        for step in range(1, chan_groups):
            chan_copy(array, step).wait_recv()
            chan_forward(array, step).start()

    pass_part(0)
    each(pass_on)
    for keep in keeps:
        keep.wait()
    own_piece.wait()

    def finish(step):
        seq_copy(step).wait_send()
        seq_forward(step).wait()

    each(finish)
    tile = math.gcd(height, 128)
    for array, (_, whole, _, lines) in enumerate(parts):
        if array + 1 < len(parts):
            pass_part(array + 1)
        for step in range(chan_groups):
            chan_forward(array, step).wait()
        store(array).start()
        target, first = (projected, 0) if array < 2 else (upstream, all_weights.shape[1] // 2)

        def product(index, carry):
            here = pl.ds(pl.multiple_of(array % 2 * height + index * tile, tile), tile)
            target[here] = jnp.dot(
                whole[here], all_weights[:, first:], preferred_element_type=jnp.float32
            )
            return carry

        lax.fori_loop(0, height // tile, product, 0)
    for array in range(4):
        store(array).wait()
        for step in range(1, chan_groups):
            chan_copy(array, step).wait_send()


def gathered(tokens, grads, weights):
    devices_seq, devices_chan = lax.axis_size("seq"), lax.axis_size("chan")
    dma = pltpu.SemaphoreType.DMA
    seq_groups, chan_groups = devices_seq // 2, devices_chan // 2
    vmem, anywhere = pl.BlockSpec(memory_space=pltpu.VMEM), pl.BlockSpec(memory_space=pl.ANY)
    wide = jax.ShapeDtypeStruct((tokens.shape[0], tokens.shape[1] * devices_chan), tokens.dtype)
    tall = jax.ShapeDtypeStruct((weights.shape[0] * devices_seq, weights.shape[1]), weights.dtype)
    return pl.pallas_call(
        functools.partial(gather_kernel, devices_seq, devices_chan),
        out_shape=(
            wide,
            wide,
            jax.ShapeDtypeStruct((tokens.shape[0], weights.shape[1]), jnp.float32),
            jax.ShapeDtypeStruct((tokens.shape[0], weights.shape[1] // 2), jnp.float32),
        ),
        in_specs=[vmem] * 3,
        out_specs=(anywhere, anywhere, vmem, vmem),
        scratch_shapes=[
            pltpu.VMEM(wide.shape, wide.dtype),
            pltpu.VMEM(wide.shape, wide.dtype),
            pltpu.VMEM(tall.shape, tall.dtype),
            dma((5,)),
            dma((4,)),
        ]
        + [dma((4, chan_groups))] * 4
        + [dma((seq_groups,))] * 4,
        compiler_params=pltpu.CompilerParams(collective_id=0, has_side_effects=True),
        name="gather_inputs",
    )(tokens, grads, weights)


def reduce_kernel(
    devices_seq,
    tile,
    state,
    rate,
    weight,
    inner,
    value,
    gate,
    early_in,
    early_out,
    tokens_hbm,
    grads_hbm,
    total,
    tokens,
    grads,
    states,
    late,
    parts,
    near,
    paired,
    far,
    load_sem,
    state_send,
    state_recv,
    pair_send,
    pair_recv,
    far_send,
    far_recv,
):
    seq, chan = lax.axis_index("seq"), lax.axis_index("chan")
    groups = devices_seq // 2
    group, parity = seq // 2, seq % 2
    rows, channels = inner.shape
    owned = near.shape[2]
    loads = [
        pltpu.make_async_copy(tokens_hbm, tokens, load_sem.at[0]),
        pltpu.make_async_copy(grads_hbm, grads, load_sem.at[1]),
    ]
    for load in loads:
        load.start()
    greet(devices_seq, 0, "all")

    def loop(start, stop, call):
        def body(step, carry):
            call(step)
            return carry

        lax.fori_loop(start, stop, body, 0)

    def state_copy(step):
        there = lax.rem(seq + step, devices_seq)
        return remote(
            state, states.at[step], state_send.at[step], state_recv.at[step], (there, chan)
        )

    def member(step):
        return lax.rem(group + step, groups)

    def piece(half, index):
        return parts.at[half, pl.ds(pl.multiple_of(index * owned, owned), owned)]

    def pair_copy(half, step):
        return remote(
            piece(half, member(step) * 2 + 1 - parity),
            near.at[half, step],
            pair_send.at[half, step],
            pair_recv.at[half, step],
            (group * 2 + 1 - parity, chan),
        )

    def far_copy(half, step):
        return remote(
            paired.at[half, step],
            far.at[half, step],
            far_send.at[half, step],
            far_recv.at[half, step],
            (member(step) * 2 + parity, chan),
        )

    def summed(left, right):
        return lax.dot_general(
            left, right, (((0,), (0,)), ((), ())), preferred_element_type=jnp.float32
        )

    def span(index):
        return pl.ds(pl.multiple_of(index * tile, tile), tile)

    loop(1, devices_seq, lambda step: state_copy(step).start())
    for load in loads:
        load.wait()

    def early_tile(index):
        product = summed(tokens[:, span(index)], early_in[...])
        product += summed(grads[:, span(index)], early_out[...])
        parts[0, span(index)] = product.astype(parts.dtype)

    loop(0, tokens.shape[1] // tile, early_tile)
    loop(1, groups, lambda step: pair_copy(0, step).start())
    pair_copy(0, 0).start()

    def absorb(step, following):
        state_copy(step).wait_recv()
        gap = lax.rem(seq - step + devices_seq, devices_seq) - seq - 1
        reach = (jnp.maximum(gap, 0) * rows).astype(jnp.float32)
        present = (gap >= 0).astype(jnp.float32)
        return following + present * states[step] * jnp.exp(-reach * rate[...])

    following = lax.fori_loop(1, devices_seq, absorb, jnp.zeros(rate.shape, jnp.float32))
    entering = weight[...] * following
    rates = rate[...]
    band = math.gcd(rows, 64)

    def source_rows(index):
        here = pl.ds(pl.multiple_of(index * band, band), band)
        position = lax.broadcasted_iota(jnp.int32, (band, channels), 0) + index * band
        reach = (rows - position).astype(jnp.float32)
        source = inner[here]
        for mode in range(rates.shape[0]):
            source += entering[mode : mode + 1] * jnp.exp(-reach * rates[mode : mode + 1])
        late[here] = jnp.concatenate([source * value[here], source * gate[here]], axis=1).astype(
            late.dtype
        )

    loop(0, rows // band, source_rows)

    def late_tile(index):
        parts[1, span(index)] = summed(tokens[:, span(index)], late[...]).astype(parts.dtype)

    loop(0, tokens.shape[1] // tile, late_tile)
    loop(1, groups, lambda step: pair_copy(1, step).start())
    pair_copy(1, 0).start()

    def pair_sum(half, step):
        own = piece(half, member(step) * 2 + parity)[...].astype(jnp.float32)
        return own + near[half, step].astype(jnp.float32)

    for half in range(2):

        def pass_on(step):
            pair_copy(half, step).wait_recv()
            paired[half, step] = pair_sum(half, step).astype(paired.dtype)
            far_copy(half, step).start()

        loop(1, groups, pass_on)
    for half in range(2):
        pair_copy(half, 0).wait_recv()
        total[half] = pair_sum(half, 0)

        def collect(step):
            far_copy(half, step).wait_recv()
            total[half] += far[half, step].astype(jnp.float32)

        loop(1, groups, collect)

        def finish(step):
            pair_copy(half, step).wait_send()
            far_copy(half, step).wait_send()

        loop(1, groups, finish)
        pair_copy(half, 0).wait_send()
    loop(1, devices_seq, lambda step: state_copy(step).wait_send())


def reduced(state, rate, weight, inner, value, gate, early_in, early_out, tokens, grads, owned):
    devices_seq = lax.axis_size("seq")
    groups = devices_seq // 2
    rows, channels = inner.shape
    width = tokens.shape[1]
    wide = 2 * channels
    vmem, anywhere = pl.BlockSpec(memory_space=pltpu.VMEM), pl.BlockSpec(memory_space=pl.ANY)
    dma, half_type = pltpu.SemaphoreType.DMA, tokens.dtype
    return pl.pallas_call(
        functools.partial(reduce_kernel, devices_seq, math.gcd(width, 512)),
        out_shape=jax.ShapeDtypeStruct((2, owned, wide), jnp.float32),
        in_specs=[vmem] * 8 + [anywhere] * 2,
        out_specs=vmem,
        scratch_shapes=[pltpu.VMEM(tokens.shape, half_type)] * 2
        + [pltpu.VMEM((devices_seq,) + state.shape, jnp.float32)]
        + [pltpu.VMEM((rows, wide), half_type), pltpu.VMEM((2, width, wide), half_type)]
        + [pltpu.VMEM((2, groups, owned, wide), half_type)] * 3
        + [dma((2,)), dma((devices_seq,)), dma((devices_seq,))]
        + [dma((2, groups))] * 4,
        compiler_params=pltpu.CompilerParams(collective_id=1, has_side_effects=True),
        name="reduce_owned",
    )(state, rate, weight, inner, value, gate, early_in, early_out, tokens, grads)


def correlate_block(signal, residues, decay_length):
    rows, channels = signal.shape
    chunk = min(64, rows)
    chunks = rows // chunk
    per_filter = channels // residues.shape[1]
    rate = jnp.repeat(1.0 / decay_length, per_filter, axis=1)
    weight = jnp.repeat(residues, per_filter, axis=1) * jnp.sqrt(-jnp.expm1(-2.0 * rate))
    offset = jnp.arange(chunk, dtype=jnp.float32)
    exponent = rate.T[:, :, None] * offset
    grow = weight.T[:, :, None] * jnp.exp(exponent)
    fall = jnp.exp(-exponent)
    later = jnp.arange(chunk)[None, :] >= jnp.arange(chunk)[:, None]
    taps = jnp.einsum("cri,crj->cij", grow, fall, precision=precise)
    taps = jnp.where(later, taps, 0.0)
    pieces = signal.reshape(chunks, chunk, channels).transpose(2, 1, 0)
    both = jnp.einsum(
        "cij,cjn->cin", jnp.concatenate([taps, fall], axis=1), pieces, precision=precise
    )
    inner, sums = both[:, :chunk], both[:, chunk:]
    step = jnp.exp(-chunk * rate).T
    state = jnp.zeros_like(step)
    entering = []
    for index in reversed(range(chunks)):
        entering.append(step * state)
        state = sums[:, :, index] + step * state
    entering = jnp.stack(entering[::-1], axis=2)
    outer = jnp.einsum("cri,crn->cin", grow, entering, precision=precise)
    return (inner + outer).transpose(2, 1, 0).reshape(rows, channels), state.T, rate, weight


def local(tokens, grad_out, in_weight, out_weight, conv_out, residues, decay_length):
    local_rows = tokens.shape[0]
    channels = out_weight.shape[1]
    owned_rows = in_weight.shape[0]
    weights = jnp.concatenate([in_weight.reshape(owned_rows, 3 * channels), out_weight], axis=1)
    full_tokens, full_grads, projected, upstream = gathered(tokens, grad_out, weights)
    projected = projected[:, : 3 * channels]
    upstream = upstream[:, channels:]
    streams = lax.reduce_precision(projected, exponent_bits=8, mantissa_bits=7)
    gate_first = streams[:, :channels]
    gate_second = streams[:, channels : 2 * channels]
    value_stream = streams[:, 2 * channels :]
    conv_value = conv_out.astype(jnp.float32)
    gated = (gate_second * conv_value).astype(jnp.bfloat16)
    grad_second = (upstream * conv_value).astype(jnp.bfloat16)
    grad_conv = upstream * gate_second
    inner, state, rate, weight = correlate_block(grad_conv, residues, decay_length)
    blank = jnp.zeros_like(gated)
    owned = reduced(
        state,
        rate,
        weight,
        inner,
        value_stream,
        gate_first,
        jnp.concatenate([grad_second, blank], axis=1),
        jnp.concatenate([blank, gated], axis=1),
        full_tokens,
        full_grads,
        owned_rows,
    )
    grad_in = jnp.stack(
        [owned[1, :, :channels], owned[0, :, :channels], owned[1, :, channels:]], axis=1
    )
    return (grad_in, owned[0, :, channels:])


def solution(mesh):
    return jax.shard_map(
        local,
        mesh=mesh,
        in_specs=(
            P("seq", "chan"),
            P("seq", "chan"),
            P("seq", None, "chan"),
            P("seq", "chan"),
            P("seq", "chan"),
            P(None, "chan"),
            P(None, "chan"),
        ),
        out_specs=(P("seq", None, "chan"), P("seq", "chan")),
        check_vma=False,
    )
```
